32 devices in a mesh: slab: 2 (over x), wide: 16 (over z, y, core).
Axes of the slice: x: 2, y: 2, z: 4, core: 2. Of those that a mesh axis runs over, the one named last changes fastest.
Arguments:
- slc: bfloat16 [128, 512, 2, 512], P('wide', 'slab'), parts along dimension 1, may hold values from -10 to 10
- offsets: bfloat16 [128, 512], P('wide', 'slab'), parts along dimension 1, may hold values from -0.5 to 0.5
- row_start: int32 [128], replicated, may hold values from 0 to 127
- row_stop: int32 [128], replicated, may hold values from 385 to 512
- pairs: int32 [64, 2], replicated, may hold values from 0 to 127, as said below
Outputs:
- coherence: bfloat16 [1024, 2, 128, 128], P(('slab', 'wide')), parts along dimension 0
- flattened: float32 [1024, 2, 64], P(('slab', 'wide')), parts along dimension 0
- ramps: float32 [128, 2, 3], P(('slab', 'wide')), parts along dimension 0
The draws below stay inside these ranges and needn't reach their ends.
There are 2 independent parts, one for each index of `slab`. The reference program is written for one: setup_inputs(seed, part) draws one part's arguments, and reference() takes and returns one part's arrays. A program takes and returns all parts, laid end to end along the dimension named above; an argument that names none is the same for every part. Nothing has to cross between parts.
Inputs may be any that keep to these rules, and one draw needn't show every extreme that they name: `pairs`: each row names two different dates.
All inputs are finite; a program needn't handle non-finite values.
Results may differ from the reference program's by a relative error of at most 0.0098.
Values may be sent and summed in bfloat16 or wider, within the bound.
A program may use at most 128 MiB of HBM per device.

```python
import math
import jax
import jax.numpy as jnp
from jax import lax

DATES = 128
AZ = 512
LOOK_AZ = 16
LOOK_RG = 16
COLS = 256
PAIRS = 64
CELLS = 512


def draw_slc(key, part):
    base_key = jax.random.fold_in(key, 101)
    field_key, date_key = jax.random.split(base_key)
    speckle = jax.random.normal(field_key, (2, COLS, AZ + 2), jnp.float32)
    scatter = (speckle[:, :, :-2] + speckle[:, :, 1:-1] + speckle[:, :, 2:]) * 0.58
    across = jnp.arange(COLS, dtype=jnp.float32) / COLS - 0.5
    along = jnp.arange(AZ, dtype=jnp.float32) / AZ - 0.5
    date_keys = jax.random.split(date_key, DATES)

    def one_date(subkey):
        slope_key, phase_key, noise_key = jax.random.split(subkey, 3)
        slopes = jax.random.uniform(slope_key, (3,), jnp.float32, -4.0, 4.0)
        rotation = slopes[0] + 2.0 * math.pi * (slopes[1] * across[:, None] + slopes[2] * along[None, :])
        rotation = rotation + 0.4 * jax.random.normal(phase_key, (COLS, AZ), jnp.float32)
        noise = 0.35 * jax.random.normal(noise_key, (2, COLS, AZ), jnp.float32)
        cos_rot, sin_rot = (jnp.cos(rotation), jnp.sin(rotation))
        real_part = scatter[0] * cos_rot - scatter[1] * sin_rot + noise[0]
        imag_part = scatter[0] * sin_rot + scatter[1] * cos_rot + noise[1]
        return jnp.clip(jnp.stack([real_part, imag_part], 1), -10.0, 10.0)
    return lax.map(one_date, date_keys).astype(jnp.bfloat16)


def draw_pairs(key, part):
    first_key, second_key = jax.random.split(jax.random.fold_in(key, 23))
    first_date = jax.random.randint(first_key, (PAIRS,), 0, DATES, jnp.int32)
    gap_dates = jax.random.randint(second_key, (PAIRS,), 1, DATES, jnp.int32)
    second_date = (first_date + gap_dates) % DATES
    return jnp.stack([first_date, second_date], 1).astype(jnp.int32)


def with_ends(drawn, stream_key, least, largest):
    index_at = [jax.random.randint(jax.random.fold_in(stream_key, axis), (), 0, length) for axis, length in enumerate(drawn.shape)]
    widest = drawn.shape.index(max(drawn.shape))
    beside = index_at[:widest] + [(index_at[widest] + 1) % drawn.shape[widest]] + index_at[widest + 1:]
    return drawn.at[tuple(index_at)].set(least).at[tuple(beside)].set(largest)


def steps_of(stream_key, shape, shards, smallest, top_value):
    def one(dim, shards_of):
        steps = jax.random.uniform(jax.random.fold_in(jax.random.fold_in(stream_key, 6), dim), (shards_of,), jnp.float32, smallest / len(shards), top_value / len(shards))
        return jnp.repeat(jnp.exp(steps), shape[dim] // shards_of).reshape((-1,) + (1,) * (len(shape) - dim - 1))

    level = one(*shards[0])
    for cut in shards[1:]:
        level = level * one(*cut)
    return level


def setup_inputs(seed: int = 0, part: int = 0) -> dict:
    splits = jax.random.split(jax.random.key(seed), 6)
    own_keys = jax.random.split(jax.random.fold_in(splits[5], part), 6)
    return {
        "slc": draw_slc(jax.random.fold_in(jax.random.fold_in(splits[5], part), 71), part),
        "offsets": jnp.clip(jax.random.uniform(own_keys[1], (DATES, COLS), jnp.float32, -0.5, 0.5) * steps_of(own_keys[1], (DATES, COLS), ((0, 16),), -0.4, 0.0), -0.5, 0.5).astype(jnp.bfloat16),
        "row_start": with_ends(jax.random.randint(splits[2], (DATES,), 0, AZ // 4), jax.random.fold_in(splits[2], 1), 0, (AZ // 4) - 1).astype(jnp.int32),
        "row_stop": with_ends(jax.random.randint(splits[3], (DATES,), AZ - AZ // 4 + 1, AZ + 1), jax.random.fold_in(splits[3], 1), AZ - AZ // 4 + 1, AZ).astype(jnp.int32),
        "pairs": draw_pairs(jax.random.fold_in(splits[5], 71), part),
    }


damping = 1.0

def tables(size):
    ordinal = jnp.arange(size, dtype=jnp.int32)
    product = ordinal[:, None] * ordinal[None, :] % size
    angles = product.astype(jnp.float32) * (2.0 * math.pi / size)
    cosine = jnp.cos(angles).astype(jnp.bfloat16)
    sine_table = jnp.sin(angles).astype(jnp.bfloat16)
    forward = jnp.concatenate([jnp.concatenate([cosine, -sine_table], 1), jnp.concatenate([sine_table, cosine], 1)], 0)
    inverse = jnp.concatenate([jnp.concatenate([cosine, sine_table], 1), jnp.concatenate([-sine_table, cosine], 1)], 0)
    return (forward, inverse)

def resample(samples, shifts, start_rows, stop_rows, forward, inverse):
    date_count, columns_here = (samples.shape[0], samples.shape[1])
    row_index = jnp.arange(AZ, dtype=jnp.int32)
    valid_rows = ((row_index[None, :] >= start_rows[:, None]) & (row_index[None, :] < stop_rows[:, None])).astype(samples.dtype)
    masked = samples * valid_rows[:, None, None, :]
    stacked = masked.reshape(date_count * columns_here, 2 * AZ)
    spectrum = jnp.dot(stacked, forward, preferred_element_type=jnp.float32).astype(jnp.bfloat16)
    spectrum = lax.optimization_barrier(spectrum).astype(jnp.float32)
    frequency = jnp.where(row_index < AZ // 2, row_index, row_index - AZ).astype(jnp.float32)
    rotation = -2.0 * math.pi / AZ * frequency[None, :] * shifts.astype(jnp.float32).reshape(date_count * columns_here, 1)
    cos_rot, sin_rot = (jnp.cos(rotation), jnp.sin(rotation))
    spec_real, spec_imag = (spectrum[:, :AZ], spectrum[:, AZ:])
    turned = jnp.concatenate([spec_real * cos_rot - spec_imag * sin_rot, spec_real * sin_rot + spec_imag * cos_rot], 1).astype(jnp.bfloat16)
    restored = jnp.dot(turned, inverse, preferred_element_type=jnp.float32) * (1.0 / AZ)
    return restored.astype(jnp.bfloat16).reshape(date_count, columns_here, 2, AZ)

def coherence_cells(columns):
    date_count, columns_here = (columns.shape[0], columns.shape[1])
    range_cells = columns_here // LOOK_RG
    line_cells = AZ // LOOK_AZ
    pixels = columns.reshape(date_count, range_cells, LOOK_RG, 2, line_cells, LOOK_AZ).transpose(1, 4, 3, 0, 2, 5)
    pixels = pixels.reshape(range_cells * line_cells, 2, date_count, LOOK_RG * LOOK_AZ)
    real_part, imag_part = (pixels[:, 0], pixels[:, 1])
    stacked = jnp.concatenate([real_part, imag_part], -1)
    partner = jnp.concatenate([stacked, jnp.concatenate([-imag_part, real_part], -1)], 1)
    covariance = jnp.einsum('gdp,gep->gde', stacked.astype(jnp.float32), partner.astype(jnp.float32))
    intensity = jnp.diagonal(covariance[:, :, :date_count], axis1=1, axis2=2) + damping
    normalizer = lax.rsqrt(intensity[:, :, None] * intensity[:, None, :])
    normalizer = jnp.concatenate([normalizer, normalizer], -1)
    coherent = covariance * normalizer
    return coherent.reshape(-1, date_count, 2, date_count).transpose(0, 2, 1, 3)

def select_pairs(coherent, pairs):
    first_date, second_date = (pairs[:, 0], pairs[:, 1])
    chosen_rows = jnp.take(coherent, first_date, axis=2)
    chooser = (jnp.arange(coherent.shape[3], dtype=jnp.int32)[None, :] == second_date[:, None]).astype(jnp.float32)
    return lax.optimization_barrier(jnp.sum(chosen_rows * chooser[None, None], -1))

def cell_design(cell_index, range_cells):
    line_cells = AZ // LOOK_AZ
    line_pos = (cell_index % line_cells).astype(jnp.float32)
    range_pos = (cell_index // line_cells).astype(jnp.float32)
    across = (line_pos + 0.5) / line_cells - 0.5
    along = (range_pos + 0.5) / range_cells - 0.5
    return jnp.stack([jnp.ones_like(across), across, along], 1)

def normal_terms(interferograms, design):
    weights = 0.1 + interferograms[:, 0] ** 2 + interferograms[:, 1] ** 2
    products = jnp.stack([design[:, 0] * design[:, 0], design[:, 0] * design[:, 1], design[:, 0] * design[:, 2], design[:, 1] * design[:, 1], design[:, 1] * design[:, 2], design[:, 2] * design[:, 2]], 1)
    normal = lax.optimization_barrier(jnp.sum(products[:, :, None] * weights[:, None, :], 0)).T
    target = lax.optimization_barrier(jnp.sum((interferograms * weights[:, None, :])[..., None] * design[:, None, None, :], 0))
    return (normal, target.transpose(1, 0, 2))

def solve_three(normal, target):
    top_left, top_mid, top_right = (normal[:, 0], normal[:, 1], normal[:, 2])
    mid_mid, mid_right, low_right = (normal[:, 3], normal[:, 4], normal[:, 5])
    adjugate_00 = mid_mid * low_right - mid_right * mid_right
    adjugate_01 = top_right * mid_right - top_mid * low_right
    adjugate_02 = top_mid * mid_right - top_right * mid_mid
    adjugate_11 = top_left * low_right - top_right * top_right
    adjugate_12 = top_mid * top_right - top_left * mid_right
    adjugate_22 = top_left * mid_mid - top_mid * top_mid
    determinant = top_left * adjugate_00 + top_mid * adjugate_01 + top_right * adjugate_02
    first_rhs, second_rhs, third_rhs = (target[..., 0], target[..., 1], target[..., 2])
    first_out = adjugate_00[:, None] * first_rhs + adjugate_01[:, None] * second_rhs + adjugate_02[:, None] * third_rhs
    second_out = adjugate_01[:, None] * first_rhs + adjugate_11[:, None] * second_rhs + adjugate_12[:, None] * third_rhs
    third_out = adjugate_02[:, None] * first_rhs + adjugate_12[:, None] * second_rhs + adjugate_22[:, None] * third_rhs
    return jnp.stack([first_out, second_out, third_out], -1) / determinant[:, None, None]

def ramp_values(coefficients, design):
    return lax.optimization_barrier(jnp.sum(design[:, None, None, :] * coefficients.transpose(1, 0, 2)[None], -1))

def reference(slc, offsets, row_start, row_stop, pairs):
    forward, inverse = tables(AZ)

    def one_date(element):
        samples, shifts, start_rows, stop_rows = element
        return resample(samples[None], shifts[None], start_rows[None], stop_rows[None], forward, inverse)[0]
    resampled = lax.map(one_date, (slc, offsets, row_start, row_stop))
    range_cells = COLS // LOOK_RG

    def one_range(position):
        columns = lax.dynamic_slice_in_dim(resampled, position * LOOK_RG, LOOK_RG, 1)
        return coherence_cells(columns)
    coherent = lax.map(one_range, jnp.arange(range_cells, dtype=jnp.int32))
    coherent = coherent.reshape(CELLS, 2, DATES, DATES)
    interferograms = select_pairs(coherent, pairs)
    design = cell_design(jnp.arange(CELLS, dtype=jnp.int32), range_cells)
    normal, target = normal_terms(interferograms, design)
    coefficients = solve_three(normal, target)
    flattened = interferograms - ramp_values(coefficients, design)
    return (coherent.astype(jnp.bfloat16), flattened, coefficients)
```

```python
import functools
import math

import jax
import jax.numpy as jnp
import numpy as np
from jax import lax
from jax.experimental import pallas as pl
from jax.experimental.pallas import tpu as pltpu
from jax.sharding import PartitionSpec as P

AZ = 512
LOOK_AZ = 16
LOOK_RG = 16
RADIX = 4
PART = AZ // RADIX
LINE_CELLS = AZ // LOOK_AZ
PHASES = 4
HIGH = 8
LOW = PART // HIGH

damping = 1.0


def host_tables():
    forward, inverse = [], []
    m = np.arange(PART)
    for r in range(RADIX):
        product = ((RADIX * m + r)[:, None] * m[None, :]) % AZ
        angles = product * (2.0 * math.pi / AZ)
        cosine, sine = np.cos(angles), np.sin(angles)
        forward.append(np.block([[cosine, sine], [-sine, cosine]]))
        inverse.append(np.block([[cosine.T, -sine.T], [sine.T, cosine.T]]))
    forward = jnp.asarray(np.stack(forward), jnp.float32).astype(jnp.bfloat16)
    inverse = jnp.asarray(np.stack(inverse), jnp.float32).astype(jnp.bfloat16)
    inverse = inverse * jnp.asarray(1.0 / AZ, jnp.bfloat16)
    return forward, inverse


def split_table(dates):
    table = np.zeros((2, dates, dates, 2), np.float32)
    for q in range(2):
        table[q, np.arange(dates), np.arange(dates), q] = 1.0
    return jnp.asarray(table.reshape(2 * dates, 2 * dates)).astype(jnp.bfloat16)


def frequency_factors():
    high = np.arange(HIGH)
    high = np.where(high < HIGH // 2, high, high - HIGH) * (RADIX * LOW)
    low = np.arange(LOW) * RADIX
    rest = np.concatenate([np.arange(RADIX), np.zeros(4)])
    factors = np.concatenate([high, low, rest]).astype(np.float32)
    return jnp.asarray(factors[:, None])


def resample_kernel(
    n, slc_ref, placed_ref, split_ref, forward_ref, inverse_ref, factor_ref, start_ref, stop_ref,
    out_ref, held, shifts, theta, mask, send_sem, recv_sem, osend_sem, orecv_sem, own_sem,
):
    me = lax.axis_index("wide")
    dates_here = slc_ref.shape[0]
    dates = held.shape[0]
    columns = held.shape[1]
    step = columns // PHASES
    barrier = pltpu.get_barrier_semaphore()

    def other(k):
        return lax.rem(me + k, n)

    def greet(k, carry):
        pl.semaphore_signal(barrier, inc=1, device_id={"wide": other(k)}, device_id_type=pl.DeviceIdType.MESH)
        return carry

    lax.fori_loop(1, n, greet, 0)
    mine = pl.ds(me * dates_here, dates_here)
    own = pltpu.make_async_copy(
        slc_ref.at[:, pl.ds(me * columns, columns)], held.at[mine], own_sem.at[0]
    )
    own.start()
    own_shift = pltpu.make_async_copy(placed_ref.at[me], shifts.at[me], own_sem.at[1])
    own_shift.start()

    row = lax.broadcasted_iota(jnp.int32, (dates, AZ), 1)
    valid = (row >= start_ref[...]) & (row < stop_ref[...])
    mask[...] = jnp.where(valid, 1.0, 0.0)
    pl.semaphore_wait(barrier, n - 1)

    def shift_copy(k):
        return pltpu.make_async_remote_copy(
            src_ref=placed_ref.at[other(k)], dst_ref=shifts.at[me],
            send_sem=osend_sem.at[k], recv_sem=orecv_sem.at[k],
            device_id={"wide": other(k)}, device_id_type=pl.DeviceIdType.MESH,
        )

    def sample_copy(phase, k):
        return pltpu.make_async_remote_copy(
            src_ref=slc_ref.at[:, pl.ds(other(k) * columns + phase * step, step)],
            dst_ref=held.at[mine, pl.ds(phase * step, step)],
            send_sem=send_sem.at[phase, k], recv_sem=recv_sem.at[phase, k],
            device_id={"wide": other(k)}, device_id_type=pl.DeviceIdType.MESH,
        )

    def start_shift(k, carry):
        shift_copy(k).start()
        return carry

    lax.fori_loop(1, n, start_shift, 0)

    def start_sample(i, carry):
        sample_copy(i // (n - 1), i % (n - 1) + 1).start()
        return carry

    lax.fori_loop(0, PHASES * (n - 1), start_sample, 0)
    own.wait()
    own_shift.wait()

    def wait_shift(k, carry):
        shift_copy(k).wait()
        return carry

    lax.fori_loop(1, n, wait_shift, 0)
    total = jnp.sum(shifts[...].astype(jnp.float32), 0)
    theta[...] = total * (-2.0 * math.pi / AZ)

    def column_pair(pair, carry):
        parts = [[] for _ in range(RADIX)]
        for side in range(2):
            column = pair * 2 + side
            packed = jnp.concatenate(
                [held[:, column, j].reshape(2 * dates, PART) for j in range(RADIX)], 1
            )
            samples = jnp.dot(split_ref[...], packed, preferred_element_type=jnp.float32)
            real = samples[:dates] * mask[...]
            imag = samples[dates:] * mask[...]
            a = [real[:, j * PART : (j + 1) * PART] for j in range(RADIX)]
            b = [imag[:, j * PART : (j + 1) * PART] for j in range(RADIX)]
            ap, am, bp, bm = a[0] + a[2], a[0] - a[2], b[0] + b[2], b[0] - b[2]
            cp, cm, dp, dm = a[1] + a[3], a[1] - a[3], b[1] + b[3], b[1] - b[3]
            groups = ((ap + cp, bp + dp), (am + dm, bm - cm), (ap - cp, bp - dp), (am - dm, bm + cm))
            for r in range(RADIX):
                parts[r].append(jnp.concatenate(groups[r], 1).astype(jnp.bfloat16))
        angle = jnp.concatenate(
            [theta[pl.ds(pair * 2, 1), :], theta[pl.ds(pair * 2 + 1, 1), :]], 1
        )
        wide = angle.shape[1]
        rotation = factor_ref[...] * angle
        cosine, sine = jnp.cos(rotation), jnp.sin(rotation)
        hc, hs = cosine[:HIGH][:, None, :], sine[:HIGH][:, None, :]
        lc, ls = cosine[HIGH : HIGH + LOW][None], sine[HIGH : HIGH + LOW][None]
        base_cos = (hc * lc - hs * ls).reshape(PART, wide)
        base_sin = (hc * ls + hs * lc).reshape(PART, wide)
        restored = []
        for r in range(RADIX):
            spectrum = lax.dot_general(
                forward_ref[r], jnp.concatenate(parts[r], 0), (((1,), (1,)), ((), ())),
                preferred_element_type=jnp.float32,
            )
            at = HIGH + LOW + r
            rc, rs = cosine[at : at + 1], sine[at : at + 1]
            if r == 0:
                turn_cos, turn_sin = base_cos, base_sin
            else:
                turn_cos = base_cos * rc - base_sin * rs
                turn_sin = base_cos * rs + base_sin * rc
            sr, si = spectrum[:PART], spectrum[PART:]
            turned = jnp.concatenate(
                [sr * turn_cos - si * turn_sin, sr * turn_sin + si * turn_cos], 0
            ).astype(jnp.bfloat16)
            restored.append(jnp.dot(inverse_ref[r], turned, preferred_element_type=jnp.float32))
        x = [v[:PART] for v in restored]
        y = [v[PART:] for v in restored]
        ap, am, bp, bm = x[0] + x[2], x[0] - x[2], y[0] + y[2], y[0] - y[2]
        cp, cm, dp, dm = x[1] + x[3], x[1] - x[3], y[1] + y[3], y[1] - y[3]
        lines = ((ap + cp, bp + dp), (am - dm, bm + cm), (ap - cp, bp - dp), (am + dm, bm - cm))
        cells = PART // LOOK_AZ
        for j in range(RADIX):
            for q in range(2):
                value = lines[j][q].astype(jnp.bfloat16)
                for side in range(2):
                    place = pl.multiple_of((pair * 2 + side) * LOOK_AZ, LOOK_AZ)
                    out_ref[
                        j * cells : (j + 1) * cells, pl.ds(place, LOOK_AZ), q * dates : (q + 1) * dates
                    ] = value[:, side * dates : (side + 1) * dates].reshape(cells, LOOK_AZ, dates)
        return carry

    def one_phase(phase, carry):
        def wait_sample(k, inner):
            sample_copy(phase, k).wait()
            return inner

        lax.fori_loop(1, n, wait_sample, 0)
        lax.fori_loop(phase * (step // 2), (phase + 1) * (step // 2), column_pair, 0)
        return carry

    lax.fori_loop(0, PHASES, one_phase, 0)


def cells_kernel(first_ref, second_ref, pixels_ref, coherence_ref, chosen_ref):
    dates = pixels_ref.shape[2] // 2
    eye = lax.broadcasted_iota(jnp.int32, (dates, dates), 0) == lax.broadcasted_iota(
        jnp.int32, (dates, dates), 1
    )
    for g in range(pixels_ref.shape[0]):
        pixels = pixels_ref[g]
        gram = lax.dot_general(
            pixels, pixels, (((0,), (0,)), ((), ())), preferred_element_type=jnp.float32
        )
        real = gram[:dates, :dates] + gram[dates:, dates:]
        imag = gram[dates:, :dates] - gram[:dates, dates:]
        diagonal = jnp.where(eye, real, 0.0)
        row = lax.rsqrt(jnp.sum(diagonal, 0, keepdims=True) + damping)
        column = lax.rsqrt(jnp.sum(diagonal, 1, keepdims=True) + damping)
        scale = row * column
        for q, value in enumerate((real, imag)):
            gamma = (value * scale).astype(jnp.bfloat16)
            coherence_ref[g, q] = gamma
            picked = jnp.dot(gamma, second_ref[...], preferred_element_type=jnp.float32)
            chosen_ref[q, g : g + 1, :] = jnp.sum(picked * first_ref[...], 0, keepdims=True)


def ramps_kernel(n, chosen_ref, flat_ref, ramps_ref, sums, sum_send, sum_recv):
    me = lax.axis_index("wide")
    cells, pairs = chosen_ref.shape[1], chosen_ref.shape[2]
    barrier = pltpu.get_barrier_semaphore()

    def other(k):
        return lax.rem(me + k, n)

    def greet(k, carry):
        pl.semaphore_signal(barrier, inc=1, device_id={"wide": other(k)}, device_id_type=pl.DeviceIdType.MESH)
        return carry

    lax.fori_loop(1, n, greet, 0)
    across = (
        lax.broadcasted_iota(jnp.int32, (cells, pairs), 0).astype(jnp.float32) + 0.5
    ) / cells - 0.5
    real, imag = chosen_ref[0], chosen_ref[1]
    weights = 0.1 + real * real + imag * imag
    tilted = weights * across

    def down(value):
        return jnp.sum(value, 0, keepdims=True)

    sums[me] = jnp.concatenate(
        [
            down(weights), down(tilted), down(tilted * across),
            down(weights * real), down(tilted * real),
            down(weights * imag), down(tilted * imag),
            jnp.zeros((1, pairs), jnp.float32),
        ],
        0,
    )
    pl.semaphore_wait(barrier, n - 1)

    def sum_copy(k):
        return pltpu.make_async_remote_copy(
            src_ref=sums.at[me], dst_ref=sums.at[me],
            send_sem=sum_send.at[k], recv_sem=sum_recv.at[k],
            device_id={"wide": other(k)}, device_id_type=pl.DeviceIdType.MESH,
        )

    def start(k, carry):
        sum_copy(k).start()
        return carry

    def finish(k, carry):
        sum_copy(k).wait()
        return carry

    lax.fori_loop(1, n, start, 0)
    lax.fori_loop(1, n, finish, 0)
    plain = jnp.zeros((8, pairs), jnp.float32)
    once = plain
    twice = plain
    for source in range(n):
        along = (source + 0.5) / n - 0.5
        value = sums[source]
        plain = plain + value
        once = once + value * along
        twice = twice + value * (along * along)

    n00, n01, n11 = plain[0:1], plain[1:2], plain[2:3]
    n02, n12, n22 = once[0:1], once[1:2], twice[0:1]
    adj00 = n11 * n22 - n12 * n12
    adj01 = n02 * n12 - n01 * n22
    adj02 = n01 * n12 - n02 * n11
    adj11 = n00 * n22 - n02 * n02
    adj12 = n01 * n02 - n00 * n12
    adj22 = n00 * n11 - n01 * n01
    determinant = n00 * adj00 + n01 * adj01 + n02 * adj02
    my_along = (me.astype(jnp.float32) + 0.5) / n - 0.5
    rows = []
    for q, value in enumerate((real, imag)):
        at = 3 + 2 * q
        t0, t1, t2 = plain[at : at + 1], plain[at + 1 : at + 2], once[at : at + 1]
        b0 = (adj00 * t0 + adj01 * t1 + adj02 * t2) / determinant
        b1 = (adj01 * t0 + adj11 * t1 + adj12 * t2) / determinant
        b2 = (adj02 * t0 + adj12 * t1 + adj22 * t2) / determinant
        rows += [b0, b1, b2]
        flat_ref[:, q, :] = value - (b0 + across * b1 + my_along * b2)
    ramps_ref[...] = jnp.concatenate(rows + [jnp.zeros((2, pairs), jnp.float32)], 0)


def local(slc, offsets, row_start, row_stop, pairs):
    n = lax.axis_size("wide")
    me = lax.axis_index("wide")
    dates_here, all_columns = slc.shape[0], slc.shape[1]
    dates = row_start.shape[0]
    columns = all_columns // n
    pair_count = pairs.shape[0]
    samples = slc.reshape(dates_here, all_columns, 2, RADIX, PART).transpose(0, 1, 3, 2, 4)
    spot = jnp.arange(dates_here, dtype=jnp.int32)[:, None] + me * dates_here
    onehot = (spot == jnp.arange(dates, dtype=jnp.int32)[None, :]).astype(jnp.bfloat16)
    placed = jnp.einsum("dc,dl->cl", offsets, onehot, preferred_element_type=jnp.float32)
    placed = placed.astype(jnp.bfloat16).reshape(n, columns, dates)
    forward, inverse = host_tables()
    vmem = pl.BlockSpec(memory_space=pltpu.VMEM)
    anywhere = pl.BlockSpec(memory_space=pl.ANY)
    pixels = pl.pallas_call(
        functools.partial(resample_kernel, n),
        out_shape=jax.ShapeDtypeStruct((LINE_CELLS, columns * LOOK_AZ, 2 * dates), jnp.bfloat16),
        in_specs=[anywhere, anywhere] + [vmem] * 6,
        out_specs=vmem,
        scratch_shapes=[
            pltpu.VMEM((dates, columns, RADIX, 2, PART), jnp.bfloat16),
            pltpu.VMEM((n, columns, dates), jnp.bfloat16),
            pltpu.VMEM((columns, dates), jnp.float32),
            pltpu.VMEM((dates, AZ), jnp.float32),
            pltpu.SemaphoreType.DMA((PHASES, n)),
            pltpu.SemaphoreType.DMA((PHASES, n)),
            pltpu.SemaphoreType.DMA((n,)),
            pltpu.SemaphoreType.DMA((n,)),
            pltpu.SemaphoreType.DMA((2,)),
        ],
        compiler_params=pltpu.CompilerParams(
            collective_id=0, has_side_effects=True, vmem_limit_bytes=48 << 20
        ),
    )(
        samples, placed, split_table(dates), forward, inverse, frequency_factors(),
        row_start[:, None], row_stop[:, None],
    )

    date = jnp.arange(dates, dtype=jnp.int32)[:, None]
    first = (date == pairs[:, 0][None, :]).astype(jnp.float32)
    second = (date == pairs[:, 1][None, :]).astype(jnp.bfloat16)
    batch = 8
    coherent, chosen = pl.pallas_call(
        cells_kernel,
        grid=(LINE_CELLS // batch,),
        in_specs=[
            pl.BlockSpec((dates, pair_count), lambda i: (0, 0)),
            pl.BlockSpec((dates, pair_count), lambda i: (0, 0)),
            pl.BlockSpec((batch, columns * LOOK_AZ, 2 * dates), lambda i: (i, 0, 0)),
        ],
        out_specs=[
            pl.BlockSpec((batch, 2, dates, dates), lambda i: (i, 0, 0, 0)),
            pl.BlockSpec((2, batch, pair_count), lambda i: (0, i, 0)),
        ],
        out_shape=[
            jax.ShapeDtypeStruct((LINE_CELLS, 2, dates, dates), jnp.bfloat16),
            jax.ShapeDtypeStruct((2, LINE_CELLS, pair_count), jnp.float32),
        ],
    )(first, second, pixels)

    flattened, ramps = pl.pallas_call(
        functools.partial(ramps_kernel, n),
        in_specs=[vmem],
        out_specs=[vmem, vmem],
        out_shape=[
            jax.ShapeDtypeStruct((LINE_CELLS, 2, pair_count), jnp.float32),
            jax.ShapeDtypeStruct((8, pair_count), jnp.float32),
        ],
        scratch_shapes=[
            pltpu.VMEM((n, 8, pair_count), jnp.float32),
            pltpu.SemaphoreType.DMA((n,)),
            pltpu.SemaphoreType.DMA((n,)),
        ],
        compiler_params=pltpu.CompilerParams(collective_id=1, has_side_effects=True),
    )(chosen)
    pairs_here = pair_count // n
    own = lax.dynamic_slice_in_dim(ramps, me * pairs_here, pairs_here, 1)[:6]
    return coherent, flattened, own.T.reshape(pairs_here, 2, 3)


def solution(mesh):
    placed = (P("wide", "slab", None, None), P("wide", "slab"), P(), P(), P())
    return jax.shard_map(
        local,
        mesh=mesh,
        in_specs=placed,
        out_specs=(
            P(("slab", "wide"), None, None, None),
            P(("slab", "wide"), None, None),
            P(("slab", "wide"), None, None),
        ),
        check_vma=False,
    )
```

```python
import functools
import math

import jax
import jax.numpy as jnp
import numpy as np
from jax import lax
from jax.experimental import pallas as pl
from jax.experimental.pallas import tpu as pltpu
from jax.sharding import PartitionSpec as P

AZ = 512
LOOK_AZ = 16
LOOK_RG = 16
RADIX = 4
PART = AZ // RADIX
LINE_CELLS = AZ // LOOK_AZ
PHASES = 8
HIGH = 8
LOW = PART // HIGH

damping = 1.0


def host_tables():
    forward, inverse = [], []
    m = np.arange(PART)
    for r in range(RADIX):
        product = ((RADIX * m + r)[:, None] * m[None, :]) % AZ
        angles = product * (2.0 * math.pi / AZ)
        cosine, sine = np.cos(angles), np.sin(angles)
        forward.append(np.block([[cosine, sine], [-sine, cosine]]))
        inverse.append(np.block([[cosine.T, -sine.T], [sine.T, cosine.T]]))
    forward = jnp.asarray(np.stack(forward), jnp.float32).astype(jnp.bfloat16)
    inverse = jnp.asarray(np.stack(inverse), jnp.float32).astype(jnp.bfloat16)
    inverse = inverse * jnp.asarray(1.0 / AZ, jnp.bfloat16)
    return forward, inverse


def split_table(dates):
    table = np.zeros((2, dates, dates, 2), np.float32)
    for q in range(2):
        table[q, np.arange(dates), np.arange(dates), q] = 1.0
    return jnp.asarray(table.reshape(2 * dates, 2 * dates)).astype(jnp.bfloat16)


def frequency_factors():
    high = np.arange(HIGH)
    high = np.where(high < HIGH // 2, high, high - HIGH) * (RADIX * LOW)
    low = np.arange(LOW) * RADIX
    rest = np.concatenate([np.arange(RADIX), np.zeros(4)])
    factors = np.concatenate([high, low, rest]).astype(np.float32)
    return jnp.asarray(factors[:, None])


def stack_kernel(
    n, slc_ref, placed_ref, split_hbm, forward_hbm, inverse_hbm, factor_ref, bounds_ref, pairs_ref,
    coherence_ref, flat_ref, ramps_ref,
    held, shifts, theta, mask, pixels_ref, coherent, chosen, sums, split_ref, forward_ref, inverse_ref,
    send_sem, recv_sem, osend_sem, orecv_sem, own_sem, out_sem, sum_send, sum_recv,
):
    me = lax.axis_index("wide")
    dates_here = slc_ref.shape[0]
    dates = held.shape[0]
    columns = held.shape[1]
    step = columns // PHASES
    barrier = pltpu.get_barrier_semaphore()

    half = n // 2

    def other(k):
        inside = (k + 1) % 2
        return ((me // half + 1 - inside) % 2) * half + (me + (k - 1) // 2 + inside) % half

    def greet(k, carry):
        pl.semaphore_signal(barrier, inc=1, device_id={"wide": other(k)}, device_id_type=pl.DeviceIdType.MESH)
        return carry

    lax.fori_loop(1, n, greet, 0)
    tables = [
        pltpu.make_async_copy(source, target, own_sem.at[2 + i])
        for i, (source, target) in enumerate(
            ((split_hbm, split_ref), (forward_hbm, forward_ref), (inverse_hbm, inverse_ref))
        )
    ]
    for table in tables:
        table.start()
    mine = pl.ds(me * dates_here, dates_here)
    own = pltpu.make_async_copy(
        slc_ref.at[:, pl.ds(me * columns, columns)], held.at[mine], own_sem.at[0]
    )
    own.start()
    own_shift = pltpu.make_async_copy(placed_ref.at[me], shifts.at[me], own_sem.at[1])
    own_shift.start()

    pl.semaphore_wait(barrier, n - 1)

    def shift_copy(k):
        return pltpu.make_async_remote_copy(
            src_ref=placed_ref.at[other(k)], dst_ref=shifts.at[me],
            send_sem=osend_sem.at[k], recv_sem=orecv_sem.at[k],
            device_id={"wide": other(k)}, device_id_type=pl.DeviceIdType.MESH,
        )

    def sample_copy(phase, k):
        return pltpu.make_async_remote_copy(
            src_ref=slc_ref.at[:, pl.ds(other(k) * columns + phase * step, step)],
            dst_ref=held.at[mine, pl.ds(phase * step, step)],
            send_sem=send_sem.at[phase, k], recv_sem=recv_sem.at[phase, k],
            device_id={"wide": other(k)}, device_id_type=pl.DeviceIdType.MESH,
        )

    def start_shift(k, carry):
        shift_copy(k).start()
        return carry

    lax.fori_loop(1, n, start_shift, 0)

    def start_sample(i, carry):
        sample_copy(i // (n - 1), i % (n - 1) + 1).start()
        return carry

    lax.fori_loop(0, PHASES * (n - 1), start_sample, 0)
    eye = lax.broadcasted_iota(jnp.int32, (dates, dates), 0) == lax.broadcasted_iota(
        jnp.int32, (dates, dates), 1
    )
    bounds = [
        jnp.sum(jnp.where(eye, bounds_ref[i : i + 1, :].astype(jnp.float32), 0.0), 1, keepdims=True)
        for i in range(2)
    ]
    row = lax.broadcasted_iota(jnp.int32, (dates, AZ), 1).astype(jnp.float32)
    mask[...] = jnp.where((row >= bounds[0]) & (row < bounds[1]), 1.0, 0.0)
    own.wait()
    own_shift.wait()
    for table in tables:
        table.wait()

    def wait_shift(k, carry):
        shift_copy(k).wait()
        return carry

    lax.fori_loop(1, n, wait_shift, 0)
    total = jnp.sum(shifts[...].astype(jnp.float32), 0)
    theta[...] = total * (-2.0 * math.pi / AZ)

    def column_pair(pair, carry):
        parts = [[] for _ in range(RADIX)]
        for side in range(2):
            column = pair * 2 + side
            packed = jnp.concatenate(
                [held[:, column, j].reshape(2 * dates, PART) for j in range(RADIX)], 1
            )
            samples = jnp.dot(split_ref[...], packed, preferred_element_type=jnp.float32)
            real = samples[:dates] * mask[...]
            imag = samples[dates:] * mask[...]
            a = [real[:, j * PART : (j + 1) * PART] for j in range(RADIX)]
            b = [imag[:, j * PART : (j + 1) * PART] for j in range(RADIX)]
            ap, am, bp, bm = a[0] + a[2], a[0] - a[2], b[0] + b[2], b[0] - b[2]
            cp, cm, dp, dm = a[1] + a[3], a[1] - a[3], b[1] + b[3], b[1] - b[3]
            groups = ((ap + cp, bp + dp), (am + dm, bm - cm), (ap - cp, bp - dp), (am - dm, bm + cm))
            for r in range(RADIX):
                parts[r].append(jnp.concatenate(groups[r], 1).astype(jnp.bfloat16))
        angle = jnp.concatenate(
            [theta[pl.ds(pair * 2, 1), :], theta[pl.ds(pair * 2 + 1, 1), :]], 1
        )
        wide = angle.shape[1]
        rotation = factor_ref[...] * angle
        cosine, sine = jnp.cos(rotation), jnp.sin(rotation)
        hc, hs = cosine[:HIGH][:, None, :], sine[:HIGH][:, None, :]
        lc, ls = cosine[HIGH : HIGH + LOW][None], sine[HIGH : HIGH + LOW][None]
        base_cos = (hc * lc - hs * ls).reshape(PART, wide)
        base_sin = (hc * ls + hs * lc).reshape(PART, wide)
        restored = []
        for r in range(RADIX):
            spectrum = lax.dot_general(
                forward_ref[r], jnp.concatenate(parts[r], 0), (((1,), (1,)), ((), ())),
                preferred_element_type=jnp.float32,
            )
            at = HIGH + LOW + r
            rc, rs = cosine[at : at + 1], sine[at : at + 1]
            if r == 0:
                turn_cos, turn_sin = base_cos, base_sin
            else:
                turn_cos = base_cos * rc - base_sin * rs
                turn_sin = base_cos * rs + base_sin * rc
            sr, si = spectrum[:PART], spectrum[PART:]
            turned = jnp.concatenate(
                [sr * turn_cos - si * turn_sin, sr * turn_sin + si * turn_cos], 0
            ).astype(jnp.bfloat16)
            restored.append(jnp.dot(inverse_ref[r], turned, preferred_element_type=jnp.float32))
        x = [v[:PART] for v in restored]
        y = [v[PART:] for v in restored]
        ap, am, bp, bm = x[0] + x[2], x[0] - x[2], y[0] + y[2], y[0] - y[2]
        cp, cm, dp, dm = x[1] + x[3], x[1] - x[3], y[1] + y[3], y[1] - y[3]
        lines = ((ap + cp, bp + dp), (am - dm, bm + cm), (ap - cp, bp - dp), (am + dm, bm - cm))
        cells = PART // LOOK_AZ
        for j in range(RADIX):
            for q in range(2):
                value = lines[j][q].astype(jnp.bfloat16)
                for side in range(2):
                    place = pl.multiple_of((pair * 2 + side) * LOOK_AZ, LOOK_AZ)
                    pixels_ref[
                        j * cells : (j + 1) * cells, pl.ds(place, LOOK_AZ), q * dates : (q + 1) * dates
                    ] = value[:, side * dates : (side + 1) * dates].reshape(cells, LOOK_AZ, dates)
        return carry

    def one_phase(phase, carry):
        def wait_sample(k, inner):
            sample_copy(phase, k).wait()
            return inner

        lax.fori_loop(1, n, wait_sample, 0)
        lax.fori_loop(phase * (step // 2), (phase + 1) * (step // 2), column_pair, 0)
        return carry

    lax.fori_loop(0, PHASES, one_phase, 0)

    batch = 8
    pair_count = pairs_ref.shape[1]
    date = lax.broadcasted_iota(jnp.int32, (dates, pair_count), 0)
    first = jnp.where(date == pairs_ref[0:1, :], 1.0, 0.0)
    second = jnp.where(date == pairs_ref[1:2, :], 1.0, 0.0).astype(jnp.bfloat16)

    def result_copy(b):
        block = pl.ds(b * batch, batch)
        return pltpu.make_async_copy(coherent.at[block], coherence_ref.at[block], out_sem.at[b])

    def cell_batch(b, carry):
        picks = [[], []]
        for i in range(batch):
            g = b * batch + i
            pixels = pixels_ref[g]
            gram = lax.dot_general(
                pixels, pixels, (((0,), (0,)), ((), ())), preferred_element_type=jnp.float32
            )
            real = gram[:dates, :dates] + gram[dates:, dates:]
            imag = gram[dates:, :dates] - gram[:dates, dates:]
            diagonal = jnp.where(eye, real, 0.0)
            row_scale = lax.rsqrt(jnp.sum(diagonal, 0, keepdims=True) + damping)
            column_scale = lax.rsqrt(jnp.sum(diagonal, 1, keepdims=True) + damping)
            scale = row_scale * column_scale
            for q, value in enumerate((real, imag)):
                gamma = (value * scale).astype(jnp.bfloat16)
                coherent[g, q] = gamma
                picked = jnp.dot(gamma, second, preferred_element_type=jnp.float32)
                picks[q].append(jnp.sum(picked * first, 0, keepdims=True))
        for q in range(2):
            chosen[q, pl.ds(pl.multiple_of(b * batch, batch), batch), :] = jnp.concatenate(picks[q], 0)
        result_copy(b).start()
        return carry

    lax.fori_loop(0, LINE_CELLS // batch, cell_batch, 0)
    across = (
        lax.broadcasted_iota(jnp.int32, (LINE_CELLS, pair_count), 0).astype(jnp.float32) + 0.5
    ) / LINE_CELLS - 0.5
    real, imag = chosen[0], chosen[1]
    weights = 0.1 + real * real + imag * imag
    tilted = weights * across

    def down(value):
        return jnp.sum(value, 0, keepdims=True)

    sums[me] = jnp.concatenate(
        [
            down(weights), down(tilted), down(tilted * across),
            down(weights * real), down(tilted * real),
            down(weights * imag), down(tilted * imag),
            jnp.zeros((1, pair_count), jnp.float32),
        ],
        0,
    )
    def sum_copy(k):
        return pltpu.make_async_remote_copy(
            src_ref=sums.at[me], dst_ref=sums.at[me],
            send_sem=sum_send.at[k], recv_sem=sum_recv.at[k],
            device_id={"wide": other(k)}, device_id_type=pl.DeviceIdType.MESH,
        )

    def start_sum(k, carry):
        sum_copy(k).start()
        return carry

    def finish_sum(k, carry):
        sum_copy(k).wait()
        return carry

    lax.fori_loop(1, n, start_sum, 0)
    lax.fori_loop(1, n, finish_sum, 0)
    plain = jnp.zeros((8, pair_count), jnp.float32)
    once = plain
    twice = plain
    for source in range(n):
        along = (source + 0.5) / n - 0.5
        value = sums[source]
        plain = plain + value
        once = once + value * along
        twice = twice + value * (along * along)

    n00, n01, n11 = plain[0:1], plain[1:2], plain[2:3]
    n02, n12, n22 = once[0:1], once[1:2], twice[0:1]
    adj00 = n11 * n22 - n12 * n12
    adj01 = n02 * n12 - n01 * n22
    adj02 = n01 * n12 - n02 * n11
    adj11 = n00 * n22 - n02 * n02
    adj12 = n01 * n02 - n00 * n12
    adj22 = n00 * n11 - n01 * n01
    determinant = n00 * adj00 + n01 * adj01 + n02 * adj02
    my_along = (me.astype(jnp.float32) + 0.5) / n - 0.5
    rows = []
    for q, value in enumerate((real, imag)):
        at = 3 + 2 * q
        t0, t1, t2 = plain[at : at + 1], plain[at + 1 : at + 2], once[at : at + 1]
        b0 = (adj00 * t0 + adj01 * t1 + adj02 * t2) / determinant
        b1 = (adj01 * t0 + adj11 * t1 + adj12 * t2) / determinant
        b2 = (adj02 * t0 + adj12 * t1 + adj22 * t2) / determinant
        rows += [b0, b1, b2]
        flat_ref[:, q, :] = value - (b0 + across * b1 + my_along * b2)
    solved = jnp.concatenate(rows + [jnp.zeros((2, pair_count), jnp.float32)], 0)
    pairs_here = ramps_ref.shape[0]
    lane = lax.broadcasted_iota(jnp.int32, (8, pair_count), 1)
    line = lax.broadcasted_iota(jnp.int32, (8, pair_count), 0)
    chooser = jnp.where(lane == me * pairs_here + line, 1.0, 0.0)
    own_ramps = lax.dot_general(
        chooser, solved, (((1,), (1,)), ((), ())),
        precision=lax.Precision.HIGHEST, preferred_element_type=jnp.float32,
    )
    for q in range(2):
        ramps_ref[:, q, :] = own_ramps[:pairs_here, 3 * q : 3 * q + 3]

    def finish_result(b, carry):
        result_copy(b).wait()
        return carry

    lax.fori_loop(0, LINE_CELLS // batch, finish_result, 0)


def local(slc, offsets, row_start, row_stop, pairs):
    n = lax.axis_size("wide")
    me = lax.axis_index("wide")
    dates_here, all_columns = slc.shape[0], slc.shape[1]
    dates = row_start.shape[0]
    columns = all_columns // n
    pair_count = pairs.shape[0]
    samples = slc.reshape(dates_here, all_columns, 2, RADIX, PART).transpose(0, 1, 3, 2, 4)
    spot = jnp.arange(dates_here, dtype=jnp.int32)[:, None] + me * dates_here
    onehot = (spot == jnp.arange(dates, dtype=jnp.int32)[None, :]).astype(jnp.bfloat16)
    placed = jnp.einsum("dc,dl->cl", offsets, onehot, preferred_element_type=jnp.float32)
    placed = placed.astype(jnp.bfloat16).reshape(n, columns, dates)
    forward, inverse = host_tables()
    vmem = pl.BlockSpec(memory_space=pltpu.VMEM)
    anywhere = pl.BlockSpec(memory_space=pl.ANY)
    far = pl.BlockSpec(memory_space=pltpu.HBM)
    coherence, flattened, ramps = pl.pallas_call(
        functools.partial(stack_kernel, n),
        out_shape=[
            jax.ShapeDtypeStruct((LINE_CELLS, 2, dates, dates), jnp.bfloat16),
            jax.ShapeDtypeStruct((LINE_CELLS, 2, pair_count), jnp.float32),
            jax.ShapeDtypeStruct((pair_count // n, 2, 3), jnp.float32),
        ],
        in_specs=[anywhere] * 2 + [far] * 3 + [vmem] * 3,
        out_specs=[anywhere, vmem, vmem],
        scratch_shapes=[
            pltpu.VMEM((dates, columns, RADIX, 2, PART), jnp.bfloat16),
            pltpu.VMEM((n, columns, dates), jnp.bfloat16),
            pltpu.VMEM((columns, dates), jnp.float32),
            pltpu.VMEM((dates, AZ), jnp.float32),
            pltpu.VMEM((LINE_CELLS, columns * LOOK_AZ, 2 * dates), jnp.bfloat16),
            pltpu.VMEM((LINE_CELLS, 2, dates, dates), jnp.bfloat16),
            pltpu.VMEM((2, LINE_CELLS, pair_count), jnp.float32),
            pltpu.VMEM((n, 8, pair_count), jnp.float32),
            pltpu.VMEM((2 * dates, 2 * dates), jnp.bfloat16),
            pltpu.VMEM(forward.shape, jnp.bfloat16),
            pltpu.VMEM(inverse.shape, jnp.bfloat16),
            pltpu.SemaphoreType.DMA((PHASES, n)),
            pltpu.SemaphoreType.DMA((PHASES, n)),
            pltpu.SemaphoreType.DMA((n,)),
            pltpu.SemaphoreType.DMA((n,)),
            pltpu.SemaphoreType.DMA((5,)),
            pltpu.SemaphoreType.DMA((LINE_CELLS // 8,)),
            pltpu.SemaphoreType.DMA((n,)),
            pltpu.SemaphoreType.DMA((n,)),
        ],
        compiler_params=pltpu.CompilerParams(
            collective_id=0, has_side_effects=True, vmem_limit_bytes=48 << 20
        ),
    )(
        samples, placed, split_table(dates), forward, inverse, frequency_factors(),
        jnp.stack([row_start, row_stop]), pairs.T,
    )
    return coherence, flattened, ramps


def solution(mesh):
    placed = (P("wide", "slab", None, None), P("wide", "slab"), P(), P(), P())
    return jax.shard_map(
        local,
        mesh=mesh,
        in_specs=placed,
        out_specs=(
            P(("slab", "wide"), None, None, None),
            P(("slab", "wide"), None, None),
            P(("slab", "wide"), None, None),
        ),
        check_vma=False,
    )
```

```python
import functools
import math

import jax
import jax.numpy as jnp
from jax import lax
from jax.experimental import pallas as pl
from jax.experimental.pallas import tpu as pltpu
from jax.sharding import PartitionSpec as P

AZ = 512
LOOK_AZ = 16
LOOK_RG = 16
RADIX = 4
PART = AZ // RADIX
LINE_CELLS = AZ // LOOK_AZ
PHASES = 8
HIGH = 8
LOW = PART // HIGH

damping = 1.0


def fill_tables(split_ref, forward_ref, inverse_ref):
    shape = split_ref.shape
    dates = shape[0] // 2
    row = lax.broadcasted_iota(jnp.int32, shape, 0)
    column = lax.broadcasted_iota(jnp.int32, shape, 1)
    target = jnp.where(row < dates, 2 * row, 2 * (row - dates) + 1)
    split_ref[...] = jnp.where(column == target, 1.0, 0.0).astype(jnp.bfloat16)
    m = lax.broadcasted_iota(jnp.int32, (PART, PART), 0)
    line = lax.broadcasted_iota(jnp.int32, (PART, PART), 1)
    for r in range(RADIX):
        angle = lax.rem((RADIX * m + r) * line, AZ).astype(jnp.float32) * (2.0 * math.pi / AZ)
        cosine, sine = jnp.cos(angle), jnp.sin(angle)
        table = jnp.concatenate(
            [jnp.concatenate([cosine, sine], 1), jnp.concatenate([-sine, cosine], 1)], 0
        )
        forward_ref[r] = table.astype(jnp.bfloat16)
        inverse_ref[r] = (table.T * (1.0 / AZ)).astype(jnp.bfloat16)


def frequency_factors():
    place = lax.broadcasted_iota(jnp.int32, (HIGH + LOW + 8, 1), 0)
    high = jnp.where(place < HIGH // 2, place, place - HIGH) * (RADIX * LOW)
    low = (place - HIGH) * RADIX
    rest = place - (HIGH + LOW)
    factors = jnp.where(place < HIGH, high, jnp.where(place < HIGH + LOW, low, rest))
    return factors.astype(jnp.float32)


def stack_kernel(
    n, pair_count, slc_ref, placed_ref, small_ref,
    coherence_ref, flat_ref, ramps_ref,
    held, shifts, theta, mask, pixels_ref, coherent, chosen, sums, split_ref, forward_ref, inverse_ref,
    send_sem, recv_sem, osend_sem, orecv_sem, own_sem, out_sem, sum_send, sum_recv,
):
    me = lax.axis_index("wide")
    dates_here = slc_ref.shape[0]
    dates = held.shape[0]
    columns = held.shape[1]
    step = columns // PHASES
    barrier = pltpu.get_barrier_semaphore()

    half = n // 2

    def other(k):
        inside = (k + 1) % 2
        return ((me // half + 1 - inside) % 2) * half + (me + (k - 1) // 2 + inside) % half

    def greet(k, carry):
        pl.semaphore_signal(barrier, inc=1, device_id={"wide": other(k)}, device_id_type=pl.DeviceIdType.MESH)
        return carry

    lax.fori_loop(1, n, greet, 0)
    mine = pl.ds(me * dates_here, dates_here)
    own = pltpu.make_async_copy(
        slc_ref.at[:, pl.ds(me * columns, columns)], held.at[mine], own_sem.at[0]
    )
    own.start()
    own_shift = pltpu.make_async_copy(placed_ref.at[me], shifts.at[me], own_sem.at[1])
    own_shift.start()

    pl.semaphore_wait(barrier, n - 1)

    def shift_copy(k):
        return pltpu.make_async_remote_copy(
            src_ref=placed_ref.at[other(k)], dst_ref=shifts.at[me],
            send_sem=osend_sem.at[k], recv_sem=orecv_sem.at[k],
            device_id={"wide": other(k)}, device_id_type=pl.DeviceIdType.MESH,
        )

    def sample_copy(phase, k):
        return pltpu.make_async_remote_copy(
            src_ref=slc_ref.at[:, pl.ds(other(k) * columns + phase * step, step)],
            dst_ref=held.at[mine, pl.ds(phase * step, step)],
            send_sem=send_sem.at[phase, k], recv_sem=recv_sem.at[phase, k],
            device_id={"wide": other(k)}, device_id_type=pl.DeviceIdType.MESH,
        )

    def start_shift(k, carry):
        shift_copy(k).start()
        return carry

    lax.fori_loop(1, n, start_shift, 0)

    def start_sample(i, carry):
        sample_copy(i // (n - 1), i % (n - 1) + 1).start()
        return carry

    lax.fori_loop(0, PHASES * (n - 1), start_sample, 0)
    fill_tables(split_ref, forward_ref, inverse_ref)
    eye = lax.broadcasted_iota(jnp.int32, (dates, dates), 0) == lax.broadcasted_iota(
        jnp.int32, (dates, dates), 1
    )
    bounds = [
        jnp.sum(jnp.where(eye, small_ref[i : i + 1, :dates].astype(jnp.float32), 0.0), 1, keepdims=True)
        for i in range(2)
    ]
    row = lax.broadcasted_iota(jnp.int32, (dates, AZ), 1).astype(jnp.float32)
    mask[...] = jnp.where((row >= bounds[0]) & (row < bounds[1]), 1.0, 0.0)
    own.wait()
    own_shift.wait()
    factors = frequency_factors()

    def wait_shift(k, carry):
        shift_copy(k).wait()
        return carry

    lax.fori_loop(1, n, wait_shift, 0)
    total = jnp.sum(shifts[...].astype(jnp.float32), 0)
    theta[...] = total * (-2.0 * math.pi / AZ)

    def column_pair(pair, carry):
        parts = [[] for _ in range(RADIX)]
        for side in range(2):
            column = pair * 2 + side
            packed = jnp.concatenate(
                [held[:, column, j].reshape(2 * dates, PART) for j in range(RADIX)], 1
            )
            samples = jnp.dot(split_ref[...], packed, preferred_element_type=jnp.float32)
            real = samples[:dates] * mask[...]
            imag = samples[dates:] * mask[...]
            a = [real[:, j * PART : (j + 1) * PART] for j in range(RADIX)]
            b = [imag[:, j * PART : (j + 1) * PART] for j in range(RADIX)]
            ap, am, bp, bm = a[0] + a[2], a[0] - a[2], b[0] + b[2], b[0] - b[2]
            cp, cm, dp, dm = a[1] + a[3], a[1] - a[3], b[1] + b[3], b[1] - b[3]
            groups = ((ap + cp, bp + dp), (am + dm, bm - cm), (ap - cp, bp - dp), (am - dm, bm + cm))
            for r in range(RADIX):
                parts[r].append(jnp.concatenate(groups[r], 1).astype(jnp.bfloat16))
        angle = jnp.concatenate(
            [theta[pl.ds(pair * 2, 1), :], theta[pl.ds(pair * 2 + 1, 1), :]], 1
        )
        wide = angle.shape[1]
        rotation = factors * angle
        cosine, sine = jnp.cos(rotation), jnp.sin(rotation)
        hc, hs = cosine[:HIGH][:, None, :], sine[:HIGH][:, None, :]
        lc, ls = cosine[HIGH : HIGH + LOW][None], sine[HIGH : HIGH + LOW][None]
        base_cos = (hc * lc - hs * ls).reshape(PART, wide)
        base_sin = (hc * ls + hs * lc).reshape(PART, wide)
        restored = []
        for r in range(RADIX):
            spectrum = lax.dot_general(
                forward_ref[r], jnp.concatenate(parts[r], 0), (((1,), (1,)), ((), ())),
                preferred_element_type=jnp.float32,
            )
            at = HIGH + LOW + r
            rc, rs = cosine[at : at + 1], sine[at : at + 1]
            if r == 0:
                turn_cos, turn_sin = base_cos, base_sin
            else:
                turn_cos = base_cos * rc - base_sin * rs
                turn_sin = base_cos * rs + base_sin * rc
            sr, si = spectrum[:PART], spectrum[PART:]
            turned = jnp.concatenate(
                [sr * turn_cos - si * turn_sin, sr * turn_sin + si * turn_cos], 0
            ).astype(jnp.bfloat16)
            restored.append(jnp.dot(inverse_ref[r], turned, preferred_element_type=jnp.float32))
        x = [v[:PART] for v in restored]
        y = [v[PART:] for v in restored]
        ap, am, bp, bm = x[0] + x[2], x[0] - x[2], y[0] + y[2], y[0] - y[2]
        cp, cm, dp, dm = x[1] + x[3], x[1] - x[3], y[1] + y[3], y[1] - y[3]
        lines = ((ap + cp, bp + dp), (am - dm, bm + cm), (ap - cp, bp - dp), (am + dm, bm - cm))
        cells = PART // LOOK_AZ
        for j in range(RADIX):
            for q in range(2):
                value = lines[j][q].astype(jnp.bfloat16)
                for side in range(2):
                    place = pl.multiple_of((pair * 2 + side) * LOOK_AZ, LOOK_AZ)
                    pixels_ref[
                        j * cells : (j + 1) * cells, pl.ds(place, LOOK_AZ), q * dates : (q + 1) * dates
                    ] = value[:, side * dates : (side + 1) * dates].reshape(cells, LOOK_AZ, dates)
        return carry

    def one_phase(phase, carry):
        def wait_sample(k, inner):
            sample_copy(phase, k).wait()
            return inner

        lax.fori_loop(1, n, wait_sample, 0)
        lax.fori_loop(phase * (step // 2), (phase + 1) * (step // 2), column_pair, 0)
        return carry

    lax.fori_loop(0, PHASES, one_phase, 0)

    batch = 8
    date = lax.broadcasted_iota(jnp.int32, (dates, pair_count), 0)
    first = jnp.where(date == small_ref[2:3, :pair_count], 1.0, 0.0)
    second = jnp.where(date == small_ref[3:4, :pair_count], 1.0, 0.0).astype(jnp.bfloat16)

    def result_copy(b):
        block = pl.ds(b * batch, batch)
        return pltpu.make_async_copy(coherent.at[block], coherence_ref.at[block], out_sem.at[b])

    def cell_batch(b, carry):
        picks = [[], []]
        for i in range(batch):
            g = b * batch + i
            pixels = pixels_ref[g]
            gram = lax.dot_general(
                pixels, pixels, (((0,), (0,)), ((), ())), preferred_element_type=jnp.float32
            )
            real = gram[:dates, :dates] + gram[dates:, dates:]
            imag = gram[dates:, :dates] - gram[:dates, dates:]
            diagonal = jnp.where(eye, real, 0.0)
            row_scale = lax.rsqrt(jnp.sum(diagonal, 0, keepdims=True) + damping)
            column_scale = lax.rsqrt(jnp.sum(diagonal, 1, keepdims=True) + damping)
            scale = row_scale * column_scale
            gamma = jnp.concatenate([real * scale, imag * scale], 0).astype(jnp.bfloat16)
            picked = jnp.dot(gamma, second, preferred_element_type=jnp.float32)
            for q in range(2):
                part = slice(q * dates, (q + 1) * dates)
                coherent[g, q] = gamma[part]
                picks[q].append(jnp.sum(picked[part] * first, 0, keepdims=True))
        for q in range(2):
            chosen[q, pl.ds(pl.multiple_of(b * batch, batch), batch), :] = jnp.concatenate(picks[q], 0)
        result_copy(b).start()
        return carry

    lax.fori_loop(0, LINE_CELLS // batch, cell_batch, 0)
    across = (
        lax.broadcasted_iota(jnp.int32, (LINE_CELLS, pair_count), 0).astype(jnp.float32) + 0.5
    ) / LINE_CELLS - 0.5
    real, imag = chosen[0], chosen[1]
    weights = 0.1 + real * real + imag * imag
    tilted = weights * across

    def down(value):
        return jnp.sum(value, 0, keepdims=True)

    sums[me] = jnp.concatenate(
        [
            down(weights), down(tilted), down(tilted * across),
            down(weights * real), down(tilted * real),
            down(weights * imag), down(tilted * imag),
            jnp.zeros((1, pair_count), jnp.float32),
        ],
        0,
    )
    def sum_copy(k):
        return pltpu.make_async_remote_copy(
            src_ref=sums.at[me], dst_ref=sums.at[me],
            send_sem=sum_send.at[k], recv_sem=sum_recv.at[k],
            device_id={"wide": other(k)}, device_id_type=pl.DeviceIdType.MESH,
        )

    def start_sum(k, carry):
        sum_copy(k).start()
        return carry

    def finish_sum(k, carry):
        sum_copy(k).wait()
        return carry

    lax.fori_loop(1, n, start_sum, 0)
    lax.fori_loop(1, n, finish_sum, 0)
    plain = jnp.zeros((8, pair_count), jnp.float32)
    once = plain
    twice = plain
    for source in range(n):
        along = (source + 0.5) / n - 0.5
        value = sums[source]
        plain = plain + value
        once = once + value * along
        twice = twice + value * (along * along)

    n00, n01, n11 = plain[0:1], plain[1:2], plain[2:3]
    n02, n12, n22 = once[0:1], once[1:2], twice[0:1]
    adj00 = n11 * n22 - n12 * n12
    adj01 = n02 * n12 - n01 * n22
    adj02 = n01 * n12 - n02 * n11
    adj11 = n00 * n22 - n02 * n02
    adj12 = n01 * n02 - n00 * n12
    adj22 = n00 * n11 - n01 * n01
    determinant = n00 * adj00 + n01 * adj01 + n02 * adj02
    my_along = (me.astype(jnp.float32) + 0.5) / n - 0.5
    rows = []
    for q, value in enumerate((real, imag)):
        at = 3 + 2 * q
        t0, t1, t2 = plain[at : at + 1], plain[at + 1 : at + 2], once[at : at + 1]
        b0 = (adj00 * t0 + adj01 * t1 + adj02 * t2) / determinant
        b1 = (adj01 * t0 + adj11 * t1 + adj12 * t2) / determinant
        b2 = (adj02 * t0 + adj12 * t1 + adj22 * t2) / determinant
        rows += [b0, b1, b2]
        flat_ref[:, q, :] = value - (b0 + across * b1 + my_along * b2)
    solved = jnp.concatenate(rows + [jnp.zeros((2, pair_count), jnp.float32)], 0)
    pairs_here = ramps_ref.shape[0]
    lane = lax.broadcasted_iota(jnp.int32, (8, pair_count), 1)
    line = lax.broadcasted_iota(jnp.int32, (8, pair_count), 0)
    chooser = jnp.where(lane == me * pairs_here + line, 1.0, 0.0)
    own_ramps = lax.dot_general(
        chooser, solved, (((1,), (1,)), ((), ())),
        precision=lax.Precision.HIGHEST, preferred_element_type=jnp.float32,
    )
    for q in range(2):
        ramps_ref[:, q, :] = own_ramps[:pairs_here, 3 * q : 3 * q + 3]

    def finish_result(b, carry):
        result_copy(b).wait()
        return carry

    lax.fori_loop(0, LINE_CELLS // batch, finish_result, 0)


def local(slc, offsets, row_start, row_stop, pairs):
    n = lax.axis_size("wide")
    me = lax.axis_index("wide")
    dates_here, all_columns = slc.shape[0], slc.shape[1]
    dates = row_start.shape[0]
    columns = all_columns // n
    pair_count = pairs.shape[0]
    samples = slc.reshape(dates_here, all_columns, 2, RADIX, PART).transpose(0, 1, 3, 2, 4)
    spot = jnp.arange(dates_here, dtype=jnp.int32)[:, None] + me * dates_here
    onehot = (spot == jnp.arange(dates, dtype=jnp.int32)[None, :]).astype(jnp.bfloat16)
    placed = jnp.einsum("dc,dl->cl", offsets, onehot, preferred_element_type=jnp.float32)
    placed = placed.astype(jnp.bfloat16).reshape(n, columns, dates)
    width = max(dates, pair_count)
    small = jnp.concatenate(
        [
            jnp.pad(row_start[None], ((0, 0), (0, width - dates))),
            jnp.pad(row_stop[None], ((0, 0), (0, width - dates))),
            jnp.pad(pairs.T, ((0, 0), (0, width - pair_count))),
        ],
        0,
    )
    vmem = pl.BlockSpec(memory_space=pltpu.VMEM)
    anywhere = pl.BlockSpec(memory_space=pl.ANY)
    coherence, flattened, ramps = pl.pallas_call(
        functools.partial(stack_kernel, n, pair_count),
        out_shape=[
            jax.ShapeDtypeStruct((LINE_CELLS, 2, dates, dates), jnp.bfloat16),
            jax.ShapeDtypeStruct((LINE_CELLS, 2, pair_count), jnp.float32),
            jax.ShapeDtypeStruct((pair_count // n, 2, 3), jnp.float32),
        ],
        in_specs=[anywhere] * 2 + [vmem],
        out_specs=[anywhere, vmem, vmem],
        scratch_shapes=[
            pltpu.VMEM((dates, columns, RADIX, 2, PART), jnp.bfloat16),
            pltpu.VMEM((n, columns, dates), jnp.bfloat16),
            pltpu.VMEM((columns, dates), jnp.float32),
            pltpu.VMEM((dates, AZ), jnp.float32),
            pltpu.VMEM((LINE_CELLS, columns * LOOK_AZ, 2 * dates), jnp.bfloat16),
            pltpu.VMEM((LINE_CELLS, 2, dates, dates), jnp.bfloat16),
            pltpu.VMEM((2, LINE_CELLS, pair_count), jnp.float32),
            pltpu.VMEM((n, 8, pair_count), jnp.float32),
            pltpu.VMEM((2 * dates, 2 * dates), jnp.bfloat16),
            pltpu.VMEM((RADIX, 2 * PART, 2 * PART), jnp.bfloat16),
            pltpu.VMEM((RADIX, 2 * PART, 2 * PART), jnp.bfloat16),
            pltpu.SemaphoreType.DMA((PHASES, n)),
            pltpu.SemaphoreType.DMA((PHASES, n)),
            pltpu.SemaphoreType.DMA((n,)),
            pltpu.SemaphoreType.DMA((n,)),
            pltpu.SemaphoreType.DMA((2,)),
            pltpu.SemaphoreType.DMA((LINE_CELLS // 8,)),
            pltpu.SemaphoreType.DMA((n,)),
            pltpu.SemaphoreType.DMA((n,)),
        ],
        compiler_params=pltpu.CompilerParams(
            collective_id=0, has_side_effects=True, vmem_limit_bytes=48 << 20
        ),
    )(
        samples, placed, small,
    )
    return coherence, flattened, ramps


def solution(mesh):
    placed = (P("wide", "slab", None, None), P("wide", "slab"), P(), P(), P())
    return jax.shard_map(
        local,
        mesh=mesh,
        in_specs=placed,
        out_specs=(
            P(("slab", "wide"), None, None, None),
            P(("slab", "wide"), None, None),
            P(("slab", "wide"), None, None),
        ),
        check_vma=False,
    )
```
